256 devices in a mesh: dom: 16 (over z, core), sub: 16 (over y, x).
Axes of the slice: x: 4, y: 4, z: 8, core: 2. Of those that a mesh axis runs over, the one named last changes fastest.
Arguments:
- state: bfloat16 [262144, 256], P(('dom', 'sub')), may hold values from -6 to 6
- tile_values: float32 [256, 24, 128, 128], P(('dom', 'sub')), may hold values from 0.0003125 to 0.009375
- tile_rows: int32 [256, 24], P(('dom', 'sub')), may hold values from 0 to 7, as said below
- tile_columns: int32 [256, 24], P(('dom', 'sub')), may hold values from 0 to 7, as said below
- tile_counts: int32 [256], P(('dom', 'sub')), may hold values from 8 to 24, as said below
- send_nodes: int32 [256, 4, 256], P(('dom', 'sub')), may hold values from 0 to 1023
- face_counts: int32 [256, 4], P(('dom', 'sub')), may hold values from 0 to 256, as said below
- capacity: float32 [262144], P(('dom', 'sub')), may hold values from 0.05 to 2
- source: float32 [262144], P(('dom', 'sub')), may hold values from -12 to 12
- w_self: bfloat16 [2, 256, 256], replicated, may hold values from -0.375 to 0.375
- w_neighbour: bfloat16 [2, 256, 256], replicated, may hold values from -0.375 to 0.375
- w_out: bfloat16 [2, 256, 256], replicated, may hold values from -0.375 to 0.375
- gains: float32 [2, 2, 256], replicated, may hold values from 0.25 to 1.75
- bias: float32 [2, 256], replicated, may hold values from -3 to 3
- w_decode: float32 [256], replicated, may hold values from -0.375 to 0.375
Outputs:
- heat_level_field: float32 [262144], P(('dom', 'sub'))
- equation_defect: float32 [262144], P(('dom', 'sub'))
The draws below stay inside these ranges and needn't reach their ends.
Inputs may be any that keep to these rules, and one draw needn't show every extreme that they name: `tile_counts`: slots at or beyond a device's count are ignored; some device has all 24 slots live. `tile_rows`: slot t < 8 names tile t, in tile_columns as well. `tile_columns`: slot t < 8 names tile t, in tile_rows as well. `face_counts`: two neighbouring devices give each other the same count; the count is 0 toward a side where the slice has no neighbour; some pair of neighbours fills all 256 slots.
All inputs are finite; a program needn't handle non-finite values.
Results may differ from the reference program's by a relative error of at most 0.005.
Values may be sent and summed in bfloat16 or wider, within the bound.
A program may use at most 64 MiB of HBM per device.

```python
import math
import jax
import jax.numpy as jnp
from jax import lax

F = 256
TILE = 128
TL = 8
LAYERS = 2
ITERS = 3
NB = 24
IFACE = 256
NODE_DEV = 1024
VERTEX_NUMBER = 262144
N_DOM = 16
N_SUB = 16
DEVICES = 256


def slot_tiles(key, salt):
    drawn = jax.random.randint(jax.random.fold_in(key, salt), (DEVICES, NB), 0, TL)
    own = jnp.arange(TL, dtype=jnp.int32)[None, :] + jnp.zeros((DEVICES, 1), jnp.int32)
    return drawn.at[:, :TL].set(own).astype(jnp.int32)


def draw_tile_rows(key, part):
    return slot_tiles(key, 11)


def draw_tile_columns(key, part):
    return slot_tiles(key, 13)


def draw_tile_counts(key, part):
    counts = jax.random.randint(key, (DEVICES,), TL, NB + 1)
    fullest = jax.random.randint(jax.random.fold_in(key, 7), (), 0, DEVICES)
    return counts.at[fullest].set(NB).astype(jnp.int32)


def draw_face_counts(key, part):
    dom_edges = jax.random.randint(jax.random.fold_in(key, 1), ((N_DOM - 1) * N_SUB,), IFACE // 4, IFACE + 1)
    fullest = jax.random.randint(jax.random.fold_in(key, 3), (), 0, (N_DOM - 1) * N_SUB)
    dom_edges = dom_edges.at[fullest].set(IFACE).reshape(N_DOM - 1, N_SUB)
    sub_edges = jax.random.randint(jax.random.fold_in(key, 2), (N_DOM, N_SUB - 1), IFACE // 4, IFACE + 1)
    zero_row = jnp.zeros((1, N_SUB), jnp.int32)
    zero_column = jnp.zeros((N_DOM, 1), jnp.int32)
    toward_low = jnp.concatenate([zero_row, dom_edges], axis=0)
    toward_upper_side = jnp.concatenate([dom_edges, zero_row], axis=0)
    toward_left = jnp.concatenate([zero_column, sub_edges], axis=1)
    toward_right = jnp.concatenate([sub_edges, zero_column], axis=1)
    stacked = jnp.stack([toward_low, toward_upper_side, toward_left, toward_right], axis=-1)
    return stacked.reshape(DEVICES, 4).astype(jnp.int32)


def draw_source(key, part):
    position = jnp.arange(VERTEX_NUMBER, dtype=jnp.float32) / (VERTEX_NUMBER - 1)
    rising = 1.0 + 2.0 * position
    values = jnp.clip(jax.random.normal(key, (VERTEX_NUMBER,), jnp.float32), -4.0, 4.0)
    return values * rising


def place_ends(values, rng, low, high):
    index_at = [jax.random.randint(jax.random.fold_in(rng, axis), (), 0, length) for axis, length in enumerate(values.shape)]
    main_axis = values.shape.index(max(values.shape))
    next_to = index_at[:main_axis] + [(index_at[main_axis] + 1) % values.shape[main_axis]] + index_at[main_axis + 1:]
    return values.at[tuple(index_at)].set(low).at[tuple(next_to)].set(high)


def shard_levels(rng, shape, cuts, smallest, high):
    level = 1.0
    for dim, parts in cuts:
        heights = jax.random.uniform(jax.random.fold_in(jax.random.fold_in(rng, 6), dim), (parts,), jnp.float32, smallest / len(cuts), high / len(cuts))
        level = level * jnp.repeat(jnp.exp(heights), shape[dim] // parts).reshape((-1,) + (1,) * (len(shape) - 1 - dim))
    return level


def scatter_about(stream_key, extent, spread, limit, cuts=(), kind=jnp.bfloat16):
    values = jax.random.normal(stream_key, extent, jnp.float32) * spread
    if len(cuts) > 0:
        values = shard_levels(stream_key, extent, cuts, -0.22, 0.18) * values
    return jnp.clip(values, min=-limit, max=limit).astype(kind)


def setup_inputs(seed: int = 0) -> dict:
    key_of = jax.random.split(jax.random.key(seed), 16)
    state = scatter_about(key_of[0], (VERTEX_NUMBER, F), 1.0, 6.0, ((0, 256),))
    tile_values = jnp.clip(jnp.exp(math.log(0.009375) - 3.4011974 * jax.random.uniform(key_of[1], (DEVICES, NB, TILE, TILE), jnp.float32) ** shard_levels(key_of[1], (DEVICES, NB, TILE, TILE), ((0, 256),), -0.2, 0.2)), 0.0003125, 0.009375)
    tile_rows = draw_tile_rows(jax.random.fold_in(key_of[15], 71), 0)
    tile_columns = draw_tile_columns(jax.random.fold_in(key_of[15], 71), 0)
    tile_counts = draw_tile_counts(jax.random.fold_in(key_of[15], 71), 0)
    send_nodes = place_ends(jax.random.randint(key_of[5], (DEVICES, 4, IFACE), 0, NODE_DEV), jax.random.fold_in(key_of[5], 1), 0, NODE_DEV - 1).astype(jnp.int32)
    face_counts = draw_face_counts(jax.random.fold_in(key_of[15], 71), 0)
    capacity = jnp.clip(jnp.exp(math.log(2.0) - 3.6888794 * jax.random.uniform(key_of[7], (VERTEX_NUMBER,), jnp.float32) ** shard_levels(key_of[7], (VERTEX_NUMBER,), ((0, 256),), -0.2, 0.2)), 0.05, 2.0)
    source = draw_source(jax.random.fold_in(key_of[15], 71), 0)
    w_self = scatter_about(key_of[9], (LAYERS, F, F), F ** -0.5, 0.375)
    w_neighbour = scatter_about(key_of[10], (LAYERS, F, F), F ** -0.5, 0.375)
    w_out = scatter_about(key_of[11], (LAYERS, F, F), F ** -0.5, 0.375)
    gains = jnp.clip(1.0 + 0.15 * jax.random.normal(key_of[12], (LAYERS, 2, F), jnp.float32), 0.25, 1.75)
    bias = scatter_about(key_of[13], (LAYERS, F), 0.5, 3.0, (), jnp.float32)
    w_decode = scatter_about(key_of[14], (F,), F ** -0.5, 0.375, (), jnp.float32)
    return dict(state=state, tile_values=tile_values, tile_rows=tile_rows, tile_columns=tile_columns, tile_counts=tile_counts, send_nodes=send_nodes, face_counts=face_counts, capacity=capacity, source=source, w_self=w_self, w_neighbour=w_neighbour, w_out=w_out, gains=gains, bias=bias, w_decode=w_decode)


EXACT = lax.Precision.HIGHEST

def placement(index, live_slots, groups):
    hits = index[:, None] == jnp.arange(groups, dtype=jnp.int32)[None, :]
    return (hits & live_slots[:, None]).astype(jnp.float32)

def block_product(tiles, rows, columns, live_slots, values):
    tile_count = values.shape[0] // TILE
    blocks = values.reshape((tile_count, TILE) + values.shape[1:])
    forward = jnp.einsum('tij,tj...->ti...', tiles, blocks[columns], precision=EXACT)
    backward = jnp.einsum('tji,tj...->ti...', tiles, blocks[rows], precision=EXACT)
    place_rows = placement(rows, live_slots, tile_count)
    place_columns = placement(columns, live_slots, tile_count)
    summed = jnp.einsum('tk,t...->k...', place_rows, forward, precision=EXACT)
    summed = summed + jnp.einsum('tk,t...->k...', place_columns, backward, precision=EXACT)
    return summed.reshape(values.shape)

def partner_rows(sent):
    grid = sent.reshape((N_DOM, N_SUB) + sent.shape[1:])
    from_low = jnp.concatenate([jnp.zeros_like(grid[:1, :, 1]), grid[:-1, :, 1]], axis=0)
    from_high = jnp.concatenate([grid[1:, :, 0], jnp.zeros_like(grid[:1, :, 0])], axis=0)
    from_left = jnp.concatenate([jnp.zeros_like(grid[:, :1, 3]), grid[:, :-1, 3]], axis=1)
    from_right = jnp.concatenate([grid[:, 1:, 2], jnp.zeros_like(grid[:, :1, 2])], axis=1)
    return jnp.stack([from_low, from_high, from_left, from_right], axis=2).reshape(sent.shape)

def interface_term(values, send_nodes, live_faces):
    picked = jax.vmap(lambda field, index: field[index])(values, send_nodes)
    mask = live_faces.reshape(live_faces.shape + (1,) * (values.ndim - 2))
    sent = jnp.where(mask, picked, jnp.zeros_like(picked))
    arrived = partner_rows(sent)

    def add_one(field, index, incoming):
        flat = incoming.reshape((-1,) + field.shape[1:]).astype(jnp.float32)
        return jnp.zeros(field.shape, jnp.float32).at[index.reshape(-1)].add(flat)
    return jax.vmap(add_one)(values, send_nodes, arrived)

def inverse_sqrt_diagonal_scaling(values, gain):
    return values * lax.rsqrt(lax.optimization_barrier(jnp.mean(values * values, axis=-1, keepdims=True)) + 1e-06) * gain

def reference(state, tile_values, tile_rows, tile_columns, tile_counts, send_nodes, face_counts, capacity, source, w_self, w_neighbour, w_out, gains, bias, w_decode):
    tile_count = NODE_DEV // TILE
    live_tiles = jnp.arange(NB, dtype=jnp.int32)[None, :] < tile_counts[:, None]
    live_faces = jnp.arange(IFACE, dtype=jnp.int32)[None, None, :] < face_counts[:, :, None]

    def tile_partial_sums(pieces):
        tiles, rows, columns, live_slots = pieces
        row_part = jnp.einsum('tk,ti->ki', placement(rows, live_slots, tile_count), lax.optimization_barrier(jnp.sum(tiles, axis=2)), precision=EXACT)
        column_part = jnp.einsum('tk,ti->ki', placement(columns, live_slots, tile_count), lax.optimization_barrier(jnp.sum(tiles, axis=1)), precision=EXACT)
        return (row_part + column_part).reshape(-1)
    rowsum = lax.map(tile_partial_sums, (tile_values, tile_rows, tile_columns, live_tiles))
    rowsum = rowsum + interface_term(jnp.ones((DEVICES, NODE_DEV), jnp.float32), send_nodes, live_faces)
    tile_half = tile_values.astype(jnp.bfloat16)

    def feature_blocks(pieces):
        tiles, rows, columns, live_slots, values = pieces
        return block_product(tiles.astype(jnp.float32), rows, columns, live_slots, values.astype(jnp.float32))
    latents = state
    for layer in range(LAYERS):
        grouped = latents.reshape(DEVICES, NODE_DEV, F)
        local = lax.map(feature_blocks, (tile_half, tile_rows, tile_columns, live_tiles, grouped))
        neighbour_mean = (local + interface_term(grouped, send_nodes, live_faces)) / rowsum[:, :, None]
        neighbour_mean = neighbour_mean.reshape(VERTEX_NUMBER, F)
        scaled_own_feature = inverse_sqrt_diagonal_scaling(latents.astype(jnp.float32), gains[layer, 0]).astype(jnp.bfloat16)
        normed_neighbour = inverse_sqrt_diagonal_scaling(neighbour_mean, gains[layer, 1]).astype(jnp.bfloat16)
        linear = jnp.dot(scaled_own_feature, w_self[layer], preferred_element_type=jnp.float32)
        linear = linear + jnp.dot(normed_neighbour, w_neighbour[layer], preferred_element_type=jnp.float32) + bias[layer]
        activated = jax.nn.silu(linear).astype(jnp.bfloat16)
        update = jnp.dot(activated, w_out[layer], preferred_element_type=jnp.float32)
        latents = (latents.astype(jnp.float32) + update).astype(jnp.bfloat16)
    network_prediction = jnp.dot(latents.astype(jnp.float32), w_decode, precision=EXACT).reshape(DEVICES, NODE_DEV)
    diagonal = capacity.reshape(DEVICES, NODE_DEV) + rowsum
    scaling = 1.0 / diagonal

    def vector_block_list(pieces):
        tiles, rows, columns, live_slots, values = pieces
        return block_product(tiles, rows, columns, live_slots, values)

    def operator(vector):
        local = lax.map(vector_block_list, (tile_values, tile_rows, tile_columns, live_tiles, vector))
        return diagonal * vector - local - interface_term(vector, send_nodes, live_faces)
    heat_level_field = network_prediction
    equation_defect = source.reshape(DEVICES, NODE_DEV) - operator(network_prediction)
    scaled = scaling * equation_defect
    conjugate_heading = scaled
    residual_dot = jnp.sum(equation_defect * scaled)
    for step in range(ITERS):
        image = operator(conjugate_heading)
        descent_factor = residual_dot / jnp.sum(conjugate_heading * image)
        heat_level_field = heat_level_field + descent_factor * conjugate_heading
        equation_defect = equation_defect - descent_factor * image
        scaled = scaling * equation_defect
        following = jnp.sum(equation_defect * scaled)
        conjugate_heading = scaled + following / residual_dot * conjugate_heading
        residual_dot = following
    return (heat_level_field.reshape(VERTEX_NUMBER), equation_defect.reshape(VERTEX_NUMBER))
```

```python
import jax
import jax.numpy as jnp
from jax import lax
from jax.sharding import PartitionSpec as P

LAYERS = 2
ITERS = 3


EXACT = lax.Precision.HIGHEST


def with_halo(shard, sides, width):
    for axis, dim in sides:
        size, length = (lax.axis_size(axis), shard.shape[dim])
        up = [(i, (i + 1) % size) for i in range(size - 1)]
        down = [(j, i) for i, j in up]
        last = lax.slice_in_dim(shard, length - width, length, axis=dim)
        initial = lax.slice_in_dim(shard, 0, width, axis=dim)
        before = lax.ppermute(last, axis, up)
        after = lax.ppermute(initial, axis, down)
        shard = jnp.concatenate([before, shard, after], axis=dim)
    return shard


def placement(index, live_slots, groups):
    hits = index[:, None] == jnp.arange(groups, dtype=jnp.int32)[None, :]
    return (hits & live_slots[:, None]).astype(jnp.float32)


def inverse_sqrt_diagonal_scaling(values, gain):
    return values * lax.rsqrt(jnp.mean(values * values, axis=-1, keepdims=True) + 1e-06) * gain


def feature_faces(sent):
    dom_grown = with_halo(sent[0:2], (("dom", 0),), 1)
    sub_grown = with_halo(sent[2:4], (("sub", 0),), 1)
    return jnp.stack([dom_grown[0], dom_grown[3], sub_grown[0], sub_grown[3]])


def vector_faces(sent):
    slots = sent.shape[1]
    cells = jnp.stack(
        [
            jnp.stack([jnp.concatenate([sent[0], sent[2]]), jnp.concatenate([sent[0], sent[3]])]),
            jnp.stack([jnp.concatenate([sent[1], sent[2]]), jnp.concatenate([sent[1], sent[3]])]),
        ]
    )
    grown = with_halo(cells, (("dom", 0), ("sub", 1)), 1)
    return jnp.stack(
        [grown[0, 1, :slots], grown[3, 1, :slots], grown[1, 0, slots:], grown[1, 3, slots:]]
    )


def galerkin_weights(gram):
    matrix = [[gram(i, j) - gram(i, j + 1) for j in range(ITERS)] for i in range(ITERS)]
    right = [gram(i, 0) for i in range(ITERS)]
    for i in range(ITERS):
        for k in range(i + 1, ITERS):
            factor = matrix[i][k] / matrix[i][i]
            for j in range(k, ITERS):
                matrix[k][j] = matrix[k][j] - factor * matrix[i][j]
            right[k] = right[k] - factor * right[i]
    weights = [None] * ITERS
    for i in reversed(range(ITERS)):
        total = right[i]
        for j in range(i + 1, ITERS):
            total = total - matrix[i][j] * weights[j]
        weights[i] = total / matrix[i][i]
    return weights


def per_device(
    state,
    tile_values,
    tile_rows,
    tile_columns,
    tile_counts,
    send_nodes,
    face_counts,
    capacity,
    source,
    w_self,
    w_neighbour,
    w_out,
    gains,
    bias,
    w_decode,
):
    tiles = tile_values[0]
    rows = tile_rows[0]
    columns = tile_columns[0]
    index = send_nodes[0]
    tile_size = tiles.shape[1]
    node_count = state.shape[0]
    width = state.shape[1]
    tile_count = node_count // tile_size
    slots = index.shape[1]
    live_slots = jnp.arange(rows.shape[0], dtype=jnp.int32) < tile_counts[0]
    live_faces = jnp.arange(slots, dtype=jnp.int32)[None, :] < face_counts[0][:, None]
    flat_index = index.reshape(-1)
    place_rows = placement(rows, live_slots, tile_count)
    place_columns = placement(columns, live_slots, tile_count)
    row_part = jnp.einsum("tk,ti->ki", place_rows, jnp.sum(tiles, axis=2), precision=EXACT)
    column_part = jnp.einsum("tk,ti->ki", place_columns, jnp.sum(tiles, axis=1), precision=EXACT)
    face_weight = (
        jnp.zeros((node_count,), jnp.float32)
        .at[flat_index]
        .add(live_faces.reshape(-1).astype(jnp.float32))
    )
    rowsum = (row_part + column_part).reshape(-1) + face_weight
    tile_half = tiles.astype(jnp.bfloat16)
    latents = state
    for layer in range(LAYERS):
        sent = jnp.where(live_faces[:, :, None], latents[index], jnp.zeros((), jnp.bfloat16))
        arrived = feature_faces(sent)
        blocks = latents.reshape(tile_count, tile_size, width)
        forward = jnp.einsum(
            "tij,tjf->tif", tile_half, blocks[columns], preferred_element_type=jnp.float32
        )
        backward = jnp.einsum(
            "tji,tjf->tif", tile_half, blocks[rows], preferred_element_type=jnp.float32
        )
        local = jnp.einsum("tk,tif->kif", place_rows, forward, precision=EXACT)
        local = local + jnp.einsum("tk,tif->kif", place_columns, backward, precision=EXACT)
        coupled = (
            jnp.zeros((node_count, width), jnp.float32)
            .at[flat_index]
            .add(arrived.reshape(-1, width).astype(jnp.float32))
        )
        neighbour_mean = (local.reshape(node_count, width) + coupled) / rowsum[:, None]
        scaled_own_feature = inverse_sqrt_diagonal_scaling(
            latents.astype(jnp.float32), gains[layer, 0]
        ).astype(jnp.bfloat16)
        normed_neighbour = inverse_sqrt_diagonal_scaling(neighbour_mean, gains[layer, 1]).astype(
            jnp.bfloat16
        )
        linear = jnp.dot(scaled_own_feature, w_self[layer], preferred_element_type=jnp.float32)
        linear = (
            linear
            + jnp.dot(normed_neighbour, w_neighbour[layer], preferred_element_type=jnp.float32)
            + bias[layer]
        )
        activated = jax.nn.silu(linear).astype(jnp.bfloat16)
        update = jnp.dot(activated, w_out[layer], preferred_element_type=jnp.float32)
        latents = (latents.astype(jnp.float32) + update).astype(jnp.bfloat16)
    network_prediction = jnp.dot(latents.astype(jnp.float32), w_decode, precision=EXACT)
    diagonal = capacity + rowsum
    scaling = 1.0 / diagonal

    def couple(vector):
        sent = jnp.where(live_faces, vector[index], jnp.float32(0.0))
        arrived = vector_faces(sent)
        blocks = vector.reshape(tile_count, tile_size)
        forward = jnp.einsum("tij,tj->ti", tiles, blocks[columns], precision=EXACT)
        backward = jnp.einsum("tji,tj->ti", tiles, blocks[rows], precision=EXACT)
        local = jnp.einsum("tk,ti->ki", place_rows, forward, precision=EXACT)
        local = local + jnp.einsum("tk,ti->ki", place_columns, backward, precision=EXACT)
        coupled = jnp.zeros((node_count,), jnp.float32).at[flat_index].add(arrived.reshape(-1))
        return local.reshape(-1) + coupled

    def scaled_couple(vector):
        return scaling * couple(vector)

    first = scaling * (source - (diagonal * network_prediction - couple(network_prediction)))
    basis = [first]
    for step in range(ITERS):
        basis.append(scaled_couple(basis[-1]))
    pairs = [(i, j) for i in range(ITERS) for j in range(i, ITERS + 1)]
    sums = lax.psum(
        jnp.stack([jnp.sum(basis[i] * (diagonal * basis[j])) for i, j in pairs]), ("dom", "sub")
    )
    gram = {pair: sums[n] for n, pair in enumerate(pairs)}
    weights = galerkin_weights(lambda i, j: gram[(min(i, j), max(i, j))])
    heat_level_field = network_prediction + sum(w * v for w, v in zip(weights, basis))
    left = basis[0]
    for step in range(ITERS):
        left = left - weights[step] * (basis[step] - basis[step + 1])
    equation_defect = diagonal * left
    return (heat_level_field, equation_defect)


def solution(mesh):
    return jax.shard_map(
        per_device,
        mesh=mesh,
        in_specs=(
            P(("dom", "sub"), None),
            P(("dom", "sub"), None, None, None),
            P(("dom", "sub"), None),
            P(("dom", "sub"), None),
            P(("dom", "sub")),
            P(("dom", "sub"), None, None),
            P(("dom", "sub"), None),
            P(("dom", "sub")),
            P(("dom", "sub")),
            P(),
            P(),
            P(),
            P(),
            P(),
            P(),
        ),
        out_specs=(P(("dom", "sub")), P(("dom", "sub"))),
        check_vma=False,
    )
```

```python
import functools

import jax
import jax.numpy as jnp
from jax import lax
from jax.experimental import pallas as pl
from jax.experimental.pallas import tpu as pltpu
from jax.sharding import PartitionSpec as P

LAYERS = 2
ITERS = 3
ROUNDS = ITERS + 1
MESH = pl.DeviceIdType.MESH
F32 = jnp.float32
BF16 = jnp.bfloat16


def assemble_kernel(counts, rows, columns, tiles, high, low, total):
    groups, size = total.shape[0], total.shape[2]
    for i in range(groups):
        for j in range(groups):
            if i != j:
                total[i, j] = jnp.zeros((size, size), F32)
    for t in range(groups):
        tile = tiles[t]
        total[t, t] = tile + tile.T

    def add(t, carry):
        r, c = rows[0, t], columns[0, t]
        tile = tiles[t]
        total[r, c] += tile
        total[c, r] += tile.T
        return carry

    lax.fori_loop(groups, counts[0], add, 0)
    for i in range(groups):
        for j in range(groups):
            block = total[i, j]
            upper = block.astype(BF16)
            at = (slice(i * size, (i + 1) * size), slice(j * size, (j + 1) * size))
            high[at] = upper
            low[at] = (block - upper.astype(F32)).astype(BF16)


def assemble(tiles, rows, columns, counts, groups):
    slots, size = tiles.shape[0], tiles.shape[1]
    nodes = groups * size
    smem = pl.BlockSpec(memory_space=pltpu.SMEM)
    vmem = pl.BlockSpec(memory_space=pltpu.VMEM)
    return pl.pallas_call(
        assemble_kernel,
        out_shape=[jax.ShapeDtypeStruct((nodes, nodes), BF16)] * 2,
        in_specs=[smem, smem, smem, vmem],
        out_specs=[vmem, vmem],
        scratch_shapes=[pltpu.VMEM((groups, groups, size, size), F32)],
        compiler_params=pltpu.CompilerParams(vmem_limit_bytes=20 << 20),
        name="assemble",
    )(counts, rows, columns, tiles)


def dot(a, b):
    return jnp.dot(a, b, preferred_element_type=F32)


def parts_of(v):
    at = lax.broadcasted_iota(jnp.int32, v.shape, 0)
    first = v.astype(BF16).astype(F32)
    rest = v - first
    second = rest.astype(BF16).astype(F32)
    third = rest - second
    picked = jnp.where(at == 0, first, jnp.where(at == 1, second, jnp.where(at == 2, third, 0.0)))
    return picked.astype(BF16)


def joined(rows):
    return jnp.broadcast_to(jnp.sum(rows, axis=0, keepdims=True), rows.shape)


def spread(row):
    return jnp.broadcast_to(row, (8, row.shape[1]))


def rooted(v, gain):
    return v * lax.rsqrt(jnp.mean(v * v, axis=-1, keepdims=True) + 1e-06) * gain


def galerkin_weights(gram):
    matrix = [[gram(i, j) - gram(i, j + 1) for j in range(ITERS)] for i in range(ITERS)]
    right = [gram(i, 0) for i in range(ITERS)]
    for i in range(ITERS):
        for k in range(i + 1, ITERS):
            factor = matrix[i][k] / matrix[i][i]
            for j in range(k, ITERS):
                matrix[k][j] = matrix[k][j] - factor * matrix[i][j]
            right[k] = right[k] - factor * right[i]
    weights = [None] * ITERS
    for i in reversed(range(ITERS)):
        total = right[i]
        for j in range(i + 1, ITERS):
            total = total - matrix[i][j] * weights[j]
        weights[i] = total / matrix[i][i]
    return weights


def solve_kernel(
    n_dom,
    n_sub,
    faces,
    send_ref,
    state,
    high,
    low,
    capacity,
    source,
    w_self,
    w_neighbour,
    w_out,
    gains,
    bias,
    w_decode,
    heat_ref,
    defect_ref,
    pick,
    place,
    latents,
    own,
    inverse,
    row_out,
    row_in,
    face_out,
    face_in,
    dom_sums,
    sub_sums,
    row_send,
    row_recv,
    face_send,
    face_recv,
    dom_send,
    dom_recv,
    sub_send,
    sub_recv,
):
    dom, sub = lax.axis_index("dom"), lax.axis_index("sub")
    nodes, width = state.shape
    slots = send_ref.shape[1]
    chunk = 256
    sides = (
        (dom > 0, (dom - 1, sub)),
        (dom < n_dom - 1, (dom + 1, sub)),
        (sub > 0, (dom, sub - 1)),
        (sub < n_sub - 1, (dom, sub + 1)),
    )
    order = (2, 3, 1, 0)

    barrier = pltpu.get_barrier_semaphore()
    for r in range(1, n_dom):
        pl.semaphore_signal(barrier, inc=1, device_id=(lax.rem(dom + r, n_dom), sub), device_id_type=MESH)
    for r in range(1, n_sub):
        pl.semaphore_signal(barrier, inc=1, device_id=(dom, lax.rem(sub + r, n_sub)), device_id_type=MESH)

    position = lax.broadcasted_iota(jnp.int32, (8, slots), 1)
    for k in range(4):
        wanted = jnp.broadcast_to(send_ref[k : k + 1, :], (8, slots))
        wanted = jnp.where(position < faces[0, k], wanted, -1).astype(F32)
        node = lax.broadcasted_iota(jnp.int32, (nodes, slots), 0).astype(F32)
        place[:, k * slots : (k + 1) * slots] = (
            jnp.where(node == wanted[0:1, :], 1.0, 0.0).astype(BF16)
        )
        upright = wanted.T[:, 0:1]
        node = lax.broadcasted_iota(jnp.int32, (slots, nodes), 1).astype(F32)
        pick[k * slots : (k + 1) * slots, :] = jnp.where(node == upright, 1.0, 0.0).astype(BF16)

    for k, (there, _) in enumerate(sides):

        @pl.when(jnp.logical_not(there))
        def _():
            for layer in range(LAYERS):
                row_in[layer, k] = jnp.zeros((slots, width), BF16)
            for step in range(ROUNDS):
                face_in[step, k] = jnp.zeros((1, slots), F32)

    def row_copy(layer, k):
        return pltpu.make_async_remote_copy(
            src_ref=row_out.at[layer, k],
            dst_ref=row_in.at[layer, k ^ 1],
            send_sem=row_send.at[layer, k],
            recv_sem=row_recv.at[layer, k ^ 1],
            device_id=sides[k][1],
            device_id_type=MESH,
        )

    def row_arrival(layer, k):
        return pltpu.make_async_remote_copy(
            src_ref=row_out.at[layer, k],
            dst_ref=row_in.at[layer, k],
            send_sem=row_send.at[layer, k],
            recv_sem=row_recv.at[layer, k],
            device_id=sides[k][1],
            device_id_type=MESH,
        )

    def face_copy(step, k):
        return pltpu.make_async_remote_copy(
            src_ref=face_out.at[step, k],
            dst_ref=face_in.at[step, k ^ 1],
            send_sem=face_send.at[step, k],
            recv_sem=face_recv.at[step, k ^ 1],
            device_id=sides[k][1],
            device_id_type=MESH,
        )

    def face_arrival(step, k):
        return pltpu.make_async_remote_copy(
            src_ref=face_out.at[step, k],
            dst_ref=face_in.at[step, k],
            send_sem=face_send.at[step, k],
            recv_sem=face_recv.at[step, k],
            device_id=sides[k][1],
            device_id_type=MESH,
        )

    for layer in range(LAYERS):
        now = state if layer == 0 else latents
        for k in order:
            row_out[layer, k] = dot(pick[k * slots : (k + 1) * slots, :], now[...]).astype(BF16)
            if layer == 0 and k == order[0]:
                pl.semaphore_wait(barrier, n_dom + n_sub - 2)

            @pl.when(sides[k][0])
            def _():
                row_copy(layer, k).start()

        if layer == 0:
            ones = jnp.ones((nodes, 128), BF16)

            def count(b, carry):
                at = pl.ds(pl.multiple_of(b * chunk, chunk), chunk)
                inverse[at, :] = 1.0 / (
                    dot(high[at, :], ones) + dot(low[at, :], ones) + dot(place[at, :], ones)
                )
                return carry

            lax.fori_loop(0, nodes // chunk, count, 0)

        def before(b, carry):
            at = pl.ds(pl.multiple_of(b * chunk, chunk), chunk)
            normed = rooted(now[at, :].astype(F32), gains[layer, 0:1, :]).astype(BF16)
            own[1, at, :] = dot(normed, w_self[layer]) + bias[layer : layer + 1, :]
            own[0, at, :] = dot(high[at, :], now[...])
            return carry

        lax.fori_loop(0, nodes // chunk, before, 0)
        for k in order:

            @pl.when(sides[k][0])
            def _():
                row_arrival(layer, k).wait_recv()

        arrived = row_in.at[layer]

        def after(b, carry):
            at = pl.ds(pl.multiple_of(b * chunk, chunk), chunk)
            coupled = own[0, at, :]
            for k in range(4):
                coupled = coupled + dot(place[at, k * slots : (k + 1) * slots], arrived[k])
            mean = coupled * jnp.concatenate([inverse[at, :]] * (width // 128), axis=1)
            normed = rooted(mean, gains[layer, 1:2, :]).astype(BF16)
            linear = own[1, at, :] + dot(normed, w_neighbour[layer])
            active = (linear / (1.0 + jnp.exp(-linear))).astype(BF16)
            latents[at, :] = (now[at, :].astype(F32) + dot(active, w_out[layer])).astype(BF16)
            return carry

        lax.fori_loop(0, nodes // chunk, after, 0)

    guess = joined(
        lax.dot_general(
            parts_of(spread(w_decode[...])),
            latents[...],
            (((1,), (1,)), ((), ())),
            preferred_element_type=F32,
        )
    )
    ones_row = jnp.ones((8, nodes), BF16)
    rowsum = dot(ones_row, high[...]) + dot(ones_row, low[...]) + dot(ones_row, pick[...])
    diagonal = spread(capacity[...]) + rowsum
    scaling = 1.0 / diagonal

    def couple(step, v):
        parts = parts_of(v)
        for k in order:
            face_out[step, k] = joined(dot(parts, place[:, k * slots : (k + 1) * slots]))[0:1, :]

            @pl.when(sides[k][0])
            def _():
                face_copy(step, k).start()

        local = dot(parts, high[...]) + dot(parts, low[...])
        for k in order:

            @pl.when(sides[k][0])
            def _():
                face_arrival(step, k).wait_recv()

        for k in range(4):
            local = local + dot(parts_of(spread(face_in[step, k])), pick[k * slots : (k + 1) * slots, :])
        return joined(local)

    first = scaling * (spread(source[...]) - (diagonal * guess - couple(0, guess)))
    basis = [first]
    for step in range(1, ROUNDS):
        basis.append(scaling * couple(step, basis[-1]))

    pairs = [(i, j) for i in range(ITERS) for j in range(i, ROUNDS)]
    at_row = lax.broadcasted_iota(jnp.int32, (16, 128), 0)
    at_lane = lax.broadcasted_iota(jnp.int32, (16, 128), 1)
    packed = jnp.zeros((16, 128), F32)
    weighted = [diagonal * v for v in basis]
    for n, (i, j) in enumerate(pairs):
        product = basis[i] * weighted[j]
        lanes = sum(product[0:1, c * 128 : (c + 1) * 128] for c in range(nodes // 128))
        packed = jnp.where(at_row == n, lanes, packed)
    packed = jnp.sum(packed, axis=1, keepdims=True)
    mine = jnp.sum(jnp.where(at_row == at_lane, packed, 0.0), axis=0, keepdims=True)

    dom_sums[dom] = mine

    def dom_copy(r):
        return pltpu.make_async_remote_copy(
            src_ref=dom_sums.at[dom],
            dst_ref=dom_sums.at[dom],
            send_sem=dom_send.at[r],
            recv_sem=dom_recv.at[r],
            device_id=(lax.rem(dom + r, n_dom), sub),
            device_id_type=MESH,
        )

    def sub_copy(r):
        return pltpu.make_async_remote_copy(
            src_ref=sub_sums.at[sub],
            dst_ref=sub_sums.at[sub],
            send_sem=sub_send.at[r],
            recv_sem=sub_recv.at[r],
            device_id=(dom, lax.rem(sub + r, n_sub)),
            device_id_type=MESH,
        )

    for r in range(1, n_dom):
        dom_copy(r).start()
    for r in range(1, n_dom):
        dom_copy(r).wait()
    sub_sums[sub] = jnp.sum(dom_sums[...], axis=0)
    for r in range(1, n_sub):
        sub_copy(r).start()
    for r in range(1, n_sub):
        sub_copy(r).wait()
    sums = jnp.sum(sub_sums[...], axis=0)

    lane = lax.broadcasted_iota(jnp.int32, (1, 128), 1)
    gram = {
        pair: jnp.sum(jnp.where(lane == n, sums, 0.0), axis=1, keepdims=True)
        for n, pair in enumerate(pairs)
    }
    weights = galerkin_weights(lambda i, j: gram[(min(i, j), max(i, j))])
    field, left = guess[0:1, :], basis[0][0:1, :]
    for step in range(ITERS):
        field = field + weights[step] * basis[step][0:1, :]
        left = left - weights[step] * (basis[step][0:1, :] - basis[step + 1][0:1, :])
    heat_ref[...] = field
    defect_ref[...] = diagonal[0:1, :] * left

    for k in order:

        @pl.when(sides[k][0])
        def _():
            for layer in range(LAYERS):
                row_copy(layer, k).wait_send()
            for step in range(ROUNDS):
                face_copy(step, k).wait_send()


def per_device(
    n_dom,
    n_sub,
    state,
    tile_values,
    tile_rows,
    tile_columns,
    tile_counts,
    send_nodes,
    face_counts,
    capacity,
    source,
    w_self,
    w_neighbour,
    w_out,
    gains,
    bias,
    w_decode,
):
    nodes, width = state.shape
    slots = send_nodes.shape[2]
    groups = nodes // tile_values.shape[2]
    high, low = assemble(tile_values[0], tile_rows, tile_columns, tile_counts, groups)
    smem = pl.BlockSpec(memory_space=pltpu.SMEM)
    vmem = pl.BlockSpec(memory_space=pltpu.VMEM)
    dma = pltpu.SemaphoreType.DMA
    heat, defect = pl.pallas_call(
        functools.partial(solve_kernel, n_dom, n_sub),
        out_shape=[jax.ShapeDtypeStruct((1, nodes), F32)] * 2,
        in_specs=[smem] + [vmem] * 12,
        out_specs=[vmem, vmem],
        scratch_shapes=[
            pltpu.VMEM((4 * slots, nodes), BF16),
            pltpu.VMEM((nodes, 4 * slots), BF16),
            pltpu.VMEM((nodes, width), BF16),
            pltpu.VMEM((2, nodes, width), F32),
            pltpu.VMEM((nodes, 128), F32),
            pltpu.VMEM((LAYERS, 4, slots, width), BF16),
            pltpu.VMEM((LAYERS, 4, slots, width), BF16),
            pltpu.VMEM((ROUNDS, 4, 1, slots), F32),
            pltpu.VMEM((ROUNDS, 4, 1, slots), F32),
            pltpu.VMEM((n_dom, 1, 128), F32),
            pltpu.VMEM((n_sub, 1, 128), F32),
            dma((LAYERS, 4)),
            dma((LAYERS, 4)),
            dma((ROUNDS, 4)),
            dma((ROUNDS, 4)),
            dma((n_dom,)),
            dma((n_dom,)),
            dma((n_sub,)),
            dma((n_sub,)),
        ],
        compiler_params=pltpu.CompilerParams(
            collective_id=0, has_side_effects=True, vmem_limit_bytes=32 << 20
        ),
        name="solve",
    )(
        face_counts,
        send_nodes[0],
        state,
        high,
        low,
        capacity[None, :],
        source[None, :],
        w_self,
        w_neighbour,
        w_out,
        gains,
        bias,
        w_decode[None, :],
    )
    return heat[0], defect[0]


def solution(mesh):
    return jax.shard_map(
        functools.partial(per_device, mesh.shape["dom"], mesh.shape["sub"]),
        mesh=mesh,
        in_specs=(
            P(("dom", "sub"), None),
            P(("dom", "sub"), None, None, None),
            P(("dom", "sub"), None),
            P(("dom", "sub"), None),
            P(("dom", "sub")),
            P(("dom", "sub"), None, None),
            P(("dom", "sub"), None),
            P(("dom", "sub")),
            P(("dom", "sub")),
            P(),
            P(),
            P(),
            P(),
            P(),
            P(),
        ),
        out_specs=(P(("dom", "sub")), P(("dom", "sub"))),
        check_vma=False,
    )
```

```python
import functools

import jax
import jax.numpy as jnp
from jax import lax
from jax.experimental import pallas as pl
from jax.experimental.pallas import tpu as pltpu
from jax.sharding import PartitionSpec as P

LAYERS = 2
ITERS = 3
ROUNDS = ITERS + 1
VMEM_BYTES = 67_043_328
MESH = pl.DeviceIdType.MESH
F32 = jnp.float32
BF16 = jnp.bfloat16


def assemble_kernel(
    counts_hbm,
    rows_hbm,
    columns_hbm,
    tiles_hbm,
    high_hbm,
    low_hbm,
    counts,
    rows,
    columns,
    tiles,
    total,
    high,
    low,
    sem,
    out_sem,
):
    groups, size = total.shape[0], total.shape[2]
    slots = tiles.shape[0]
    cuts = [(at, min(at + groups, slots)) for at in range(0, slots, groups)]
    copies = [
        pltpu.make_async_copy(tiles_hbm.at[0, lo:hi], tiles.at[lo:hi], sem.at[n])
        for n, (lo, hi) in enumerate(cuts)
    ]
    small = [
        pltpu.make_async_copy(counts_hbm, counts, sem.at[len(cuts)]),
        pltpu.make_async_copy(rows_hbm, rows, sem.at[len(cuts) + 1]),
        pltpu.make_async_copy(columns_hbm, columns, sem.at[len(cuts) + 2]),
    ]
    for copy in copies + small:
        copy.start()
    for i in range(groups):
        for j in range(groups):
            if i != j:
                total[i, j] = jnp.zeros((size, size), F32)
    copies[0].wait()
    for t in range(groups):
        tile = tiles[t]
        total[t, t] = tile + tile.T
    for copy in copies[1:] + small:
        copy.wait()

    def add(t, carry):
        r, c = rows[0, t], columns[0, t]
        tile = tiles[t]
        total[r, c] += tile
        total[c, r] += tile.T
        return carry

    lax.fori_loop(groups, counts[0], add, 0)
    stores = []
    for i in range(groups):
        for j in range(groups):
            block = total[i, j]
            upper = block.astype(BF16)
            at = (slice(i * size, (i + 1) * size), slice(j * size, (j + 1) * size))
            high[at] = upper
            low[at] = (block - upper.astype(F32)).astype(BF16)
        band = slice(i * size, (i + 1) * size)
        stores.append(pltpu.make_async_copy(high.at[band], high_hbm.at[band], out_sem.at[0, i]))
        stores.append(pltpu.make_async_copy(low.at[band], low_hbm.at[band], out_sem.at[1, i]))
        stores[-2].start()
        stores[-1].start()
    for store in stores:
        store.wait()


def assemble(tiles, rows, columns, counts, groups):
    slots, size = tiles.shape[1], tiles.shape[2]
    nodes = groups * size
    hbm = pl.BlockSpec(memory_space=pltpu.HBM)
    return pl.pallas_call(
        assemble_kernel,
        out_shape=[jax.ShapeDtypeStruct((nodes, nodes), BF16)] * 2,
        in_specs=[hbm] * 4,
        out_specs=[hbm, hbm],
        scratch_shapes=[
            pltpu.SMEM(counts.shape, jnp.int32),
            pltpu.SMEM(rows.shape, jnp.int32),
            pltpu.SMEM(columns.shape, jnp.int32),
            pltpu.VMEM((slots, size, size), F32),
            pltpu.VMEM((groups, groups, size, size), F32),
            pltpu.VMEM((nodes, nodes), BF16),
            pltpu.VMEM((nodes, nodes), BF16),
            pltpu.SemaphoreType.DMA((-(-slots // groups) + 3,)),
            pltpu.SemaphoreType.DMA((2, groups)),
        ],
        compiler_params=pltpu.CompilerParams(vmem_limit_bytes=VMEM_BYTES),
        name="assemble",
    )(counts, rows, columns, tiles)


def dot(a, b):
    return jnp.dot(a, b, preferred_element_type=F32)


def parts_of(v):
    at = lax.broadcasted_iota(jnp.int32, v.shape, 0)
    first = v.astype(BF16).astype(F32)
    rest = v - first
    second = rest.astype(BF16).astype(F32)
    third = rest - second
    picked = jnp.where(at == 0, first, jnp.where(at == 1, second, jnp.where(at == 2, third, 0.0)))
    return picked.astype(BF16)


def joined(rows):
    return jnp.broadcast_to(jnp.sum(rows, axis=0, keepdims=True), rows.shape)


def spread(row):
    return jnp.broadcast_to(row, (8, row.shape[1]))


def rooted(v, gain):
    return v * lax.rsqrt(jnp.mean(v * v, axis=-1, keepdims=True) + 1e-06) * gain


def galerkin_weights(gram):
    matrix = [[gram(i, j) - gram(i, j + 1) for j in range(ITERS)] for i in range(ITERS)]
    right = [gram(i, 0) for i in range(ITERS)]
    for i in range(ITERS):
        for k in range(i + 1, ITERS):
            factor = matrix[i][k] / matrix[i][i]
            for j in range(k, ITERS):
                matrix[k][j] = matrix[k][j] - factor * matrix[i][j]
            right[k] = right[k] - factor * right[i]
    weights = [None] * ITERS
    for i in reversed(range(ITERS)):
        total = right[i]
        for j in range(i + 1, ITERS):
            total = total - matrix[i][j] * weights[j]
        weights[i] = total / matrix[i][i]
    return weights


def solve_kernel(n_dom, n_sub, *refs):
    copied, refs = refs[:13], refs[13:]
    (heat_ref, defect_ref), refs = refs[:2], refs[2:]
    local, refs = refs[:13], refs[13:]
    faces, send_ref, state, capacity, source, w_self, w_neighbour, w_out, gains, bias, w_decode = local[:11]
    high, low = local[11:]
    (
        load,
        pick,
        place,
        latents,
        own,
        inverse,
        row_out,
        row_in,
        face_out,
        face_in,
        dom_sums,
        sub_sums,
        row_send,
        row_recv,
        face_send,
        face_recv,
        dom_send,
        dom_recv,
        sub_send,
        sub_recv,
    ) = refs
    loads = [
        pltpu.make_async_copy(source_ref, target, load.at[n])
        for n, (source_ref, target) in enumerate(zip(copied, local))
    ]
    for n in (1, 0, 2, 11, 12, 5, 8, 9, 6, 7, 10, 3, 4):
        loads[n].start()
    dom, sub = lax.axis_index("dom"), lax.axis_index("sub")
    nodes, width = state.shape
    slots = send_ref.shape[1]
    chunk = 256
    sides = (
        (dom > 0, (dom - 1, sub)),
        (dom < n_dom - 1, (dom + 1, sub)),
        (sub > 0, (dom, sub - 1)),
        (sub < n_sub - 1, (dom, sub + 1)),
    )
    order = (2, 3, 1, 0)

    barrier = pltpu.get_barrier_semaphore()
    for r in range(1, n_dom):
        pl.semaphore_signal(barrier, inc=1, device_id=(lax.rem(dom + r, n_dom), sub), device_id_type=MESH)
    for r in range(1, n_sub):
        pl.semaphore_signal(barrier, inc=1, device_id=(dom, lax.rem(sub + r, n_sub)), device_id_type=MESH)

    position = lax.broadcasted_iota(jnp.int32, (8, slots), 1)
    loads[1].wait()
    loads[0].wait()
    wanted = [
        jnp.where(
            position < faces[0, k], jnp.broadcast_to(send_ref[k : k + 1, :], (8, slots)), -1
        ).astype(F32)
        for k in range(4)
    ]
    for k in order:
        node = lax.broadcasted_iota(jnp.int32, (slots, nodes), 1).astype(F32)
        upright = wanted[k].T[:, 0:1]
        pick[k * slots : (k + 1) * slots, :] = jnp.where(node == upright, 1.0, 0.0).astype(BF16)
    at_row = lax.broadcasted_iota(jnp.int32, (8, 128), 0)
    slot_node = jnp.zeros((8, 128), jnp.int32)
    for r in range(8):
        lanes = slice((r % 2) * 128, (r % 2) * 128 + 128)
        slot_node = jnp.where(at_row == r, send_ref[r // 2 : r // 2 + 1, lanes], slot_node)
    slot_lane, slot_group = jnp.bitwise_and(slot_node, 127), jnp.right_shift(slot_node, 7)
    loads[2].wait()

    for k, (there, _) in enumerate(sides):

        @pl.when(jnp.logical_not(there))
        def _():
            for layer in range(LAYERS):
                row_in[layer, k] = jnp.zeros((slots, width), BF16)
            for step in range(ROUNDS):
                face_in[step, k] = jnp.zeros((2, 128), F32)

    def row_copy(layer, k):
        return pltpu.make_async_remote_copy(
            src_ref=row_out.at[layer, k],
            dst_ref=row_in.at[layer, k ^ 1],
            send_sem=row_send.at[layer, k],
            recv_sem=row_recv.at[layer, k ^ 1],
            device_id=sides[k][1],
            device_id_type=MESH,
        )

    def row_arrival(layer, k):
        return pltpu.make_async_remote_copy(
            src_ref=row_out.at[layer, k],
            dst_ref=row_in.at[layer, k],
            send_sem=row_send.at[layer, k],
            recv_sem=row_recv.at[layer, k],
            device_id=sides[k][1],
            device_id_type=MESH,
        )

    def face_copy(step, k):
        return pltpu.make_async_remote_copy(
            src_ref=face_out.at[step, k],
            dst_ref=face_in.at[step, k ^ 1],
            send_sem=face_send.at[step, k],
            recv_sem=face_recv.at[step, k ^ 1],
            device_id=sides[k][1],
            device_id_type=MESH,
        )

    def face_arrival(step, k):
        return pltpu.make_async_remote_copy(
            src_ref=face_out.at[step, k],
            dst_ref=face_in.at[step, k],
            send_sem=face_send.at[step, k],
            recv_sem=face_recv.at[step, k],
            device_id=sides[k][1],
            device_id_type=MESH,
        )

    for layer in range(LAYERS):
        now = state if layer == 0 else latents
        for k in order:
            row_out[layer, k] = dot(pick[k * slots : (k + 1) * slots, :], now[...]).astype(BF16)
            if layer == 0 and k == order[0]:
                pl.semaphore_wait(barrier, n_dom + n_sub - 2)

            @pl.when(sides[k][0])
            def _():
                row_copy(layer, k).start()

        if layer == 0:
            for k in range(4):
                node = lax.broadcasted_iota(jnp.int32, (nodes, slots), 0).astype(F32)
                place[:, k * slots : (k + 1) * slots] = (
                    jnp.where(node == wanted[k][0:1, :], 1.0, 0.0).astype(BF16)
                )
            for n in range(3, len(loads)):
                loads[n].wait()
            ones = jnp.ones((nodes, 128), BF16)

            def count(b, carry):
                at = pl.ds(pl.multiple_of(b * chunk, chunk), chunk)
                inverse[at, :] = 1.0 / (
                    dot(high[at, :], ones) + dot(low[at, :], ones) + dot(place[at, :], ones)
                )
                return carry

            lax.fori_loop(0, nodes // chunk, count, 0)
        def before(b, carry):
            at = pl.ds(pl.multiple_of(b * chunk, chunk), chunk)
            normed = rooted(now[at, :].astype(F32), gains[layer, 0:1, :]).astype(BF16)
            own[1, at, :] = dot(normed, w_self[layer]) + bias[layer : layer + 1, :]
            own[0, at, :] = dot(high[at, :], now[...])
            return carry

        lax.fori_loop(0, nodes // chunk, before, 0)
        def arrive(k):
            @pl.when(sides[k][0])
            def _():
                row_arrival(layer, k).wait_recv()

        arrived = row_in.at[layer]

        def side(k):
            def add(b, carry):
                at = pl.ds(pl.multiple_of(b * chunk, chunk), chunk)
                own[0, at, :] += dot(place[at, k * slots : (k + 1) * slots], arrived[k])
                return carry

            lax.fori_loop(0, nodes // chunk, add, 0)

        for k in (0, 1):
            arrive(k)
            side(k)
        arrive(2)
        arrive(3)
        for b in range(nodes // chunk):
            at = slice(b * chunk, (b + 1) * chunk)
            coupled = own[0, at, :]
            for k in (2, 3):
                coupled = coupled + dot(place[at, k * slots : (k + 1) * slots], arrived[k])
            mean = coupled * jnp.concatenate([inverse[at, :]] * (width // 128), axis=1)
            normed = rooted(mean, gains[layer, 1:2, :]).astype(BF16)
            linear = own[1, at, :] + dot(normed, w_neighbour[layer])
            active = (linear / (1.0 + jnp.exp(-linear))).astype(BF16)
            latents[at, :] = (now[at, :].astype(F32) + dot(active, w_out[layer])).astype(BF16)

    guess = joined(
        lax.dot_general(
            parts_of(spread(w_decode[...])),
            latents[...],
            (((1,), (1,)), ((), ())),
            preferred_element_type=F32,
        )
    )
    ones_row = jnp.ones((8, nodes), BF16)
    rowsum = dot(ones_row, high[...]) + dot(ones_row, low[...]) + dot(ones_row, pick[...])
    diagonal = spread(capacity[...]) + rowsum
    scaling = 1.0 / diagonal

    def couple(step, v):
        sent = jnp.zeros((8, 128), F32)
        for c in range(nodes // 128):
            found = jnp.take_along_axis(v[:, c * 128 : (c + 1) * 128], slot_lane, axis=1)
            sent = jnp.where(slot_group == c, found, sent)
        for k in order:
            face_out[step, k] = sent[2 * k : 2 * k + 2, :]

            @pl.when(sides[k][0])
            def _():
                face_copy(step, k).start()

        parts = parts_of(v)
        coupled = dot(parts, high[...]) + dot(parts, low[...])
        for k in range(4):

            @pl.when(sides[k][0])
            def _():
                face_arrival(step, k).wait_recv()

            came = face_in[step, k]
            came = jnp.concatenate([spread(came[0:1, :]), spread(came[1:2, :])], axis=1)
            coupled = coupled + dot(parts_of(came), pick[k * slots : (k + 1) * slots, :])
        return joined(coupled)

    first = scaling * (spread(source[...]) - (diagonal * guess - couple(0, guess)))
    basis = [first]
    for step in range(1, ROUNDS):
        basis.append(scaling * couple(step, basis[-1]))

    pairs = [(i, j) for i in range(ITERS) for j in range(i, ROUNDS)]
    at_row = lax.broadcasted_iota(jnp.int32, (16, 128), 0)
    at_lane = lax.broadcasted_iota(jnp.int32, (16, 128), 1)
    packed = jnp.zeros((16, 128), F32)
    weighted = [diagonal * v for v in basis]
    for n, (i, j) in enumerate(pairs):
        product = basis[i] * weighted[j]
        lanes = sum(product[0:1, c * 128 : (c + 1) * 128] for c in range(nodes // 128))
        packed = jnp.where(at_row == n, lanes, packed)
    packed = jnp.sum(packed, axis=1, keepdims=True)
    mine = jnp.sum(jnp.where(at_row == at_lane, packed, 0.0), axis=0, keepdims=True)

    dom_sums[dom] = mine

    def dom_copy(r):
        return pltpu.make_async_remote_copy(
            src_ref=dom_sums.at[dom],
            dst_ref=dom_sums.at[dom],
            send_sem=dom_send.at[r],
            recv_sem=dom_recv.at[r],
            device_id=(lax.rem(dom + r, n_dom), sub),
            device_id_type=MESH,
        )

    def sub_copy(r):
        return pltpu.make_async_remote_copy(
            src_ref=sub_sums.at[sub],
            dst_ref=sub_sums.at[sub],
            send_sem=sub_send.at[r],
            recv_sem=sub_recv.at[r],
            device_id=(dom, lax.rem(sub + r, n_sub)),
            device_id_type=MESH,
        )

    for r in range(1, n_dom):
        dom_copy(r).start()
    for r in range(1, n_dom):
        dom_copy(r).wait()
    sub_sums[sub] = jnp.sum(dom_sums[...], axis=0)
    for r in range(1, n_sub):
        sub_copy(r).start()
    for r in range(1, n_sub):
        sub_copy(r).wait()
    sums = jnp.sum(sub_sums[...], axis=0)

    lane = lax.broadcasted_iota(jnp.int32, (1, 128), 1)
    gram = {
        pair: jnp.sum(jnp.where(lane == n, sums, 0.0), axis=1, keepdims=True)
        for n, pair in enumerate(pairs)
    }
    weights = galerkin_weights(lambda i, j: gram[(min(i, j), max(i, j))])
    field, left = guess[0:1, :], basis[0][0:1, :]
    for step in range(ITERS):
        field = field + weights[step] * basis[step][0:1, :]
        left = left - weights[step] * (basis[step][0:1, :] - basis[step + 1][0:1, :])
    heat_ref[...] = field
    defect_ref[...] = diagonal[0:1, :] * left

    for k in order:

        @pl.when(sides[k][0])
        def _():
            for layer in range(LAYERS):
                row_copy(layer, k).wait_send()
            for step in range(ROUNDS):
                face_copy(step, k).wait_send()


def per_device(
    n_dom,
    n_sub,
    state,
    tile_values,
    tile_rows,
    tile_columns,
    tile_counts,
    send_nodes,
    face_counts,
    capacity,
    source,
    w_self,
    w_neighbour,
    w_out,
    gains,
    bias,
    w_decode,
):
    nodes, width = state.shape
    slots = send_nodes.shape[2]
    groups = nodes // tile_values.shape[2]
    high, low = assemble(tile_values, tile_rows, tile_columns, tile_counts, groups)
    hbm = pl.BlockSpec(memory_space=pltpu.HBM)
    vmem = pl.BlockSpec(memory_space=pltpu.VMEM)
    dma = pltpu.SemaphoreType.DMA
    copied = (
        face_counts,
        send_nodes[0],
        state,
        capacity[None, :],
        source[None, :],
        w_self,
        w_neighbour,
        w_out,
        gains,
        bias,
        w_decode[None, :],
        high,
        low,
    )
    heat, defect = pl.pallas_call(
        functools.partial(solve_kernel, n_dom, n_sub),
        out_shape=[jax.ShapeDtypeStruct((1, nodes), F32)] * 2,
        in_specs=[hbm] * len(copied),
        out_specs=[vmem, vmem],
        scratch_shapes=[pltpu.SMEM(face_counts.shape, jnp.int32)]
        + [pltpu.VMEM(array.shape, array.dtype) for array in copied[1:]]
        + [
            dma((len(copied),)),
            pltpu.VMEM((4 * slots, nodes), BF16),
            pltpu.VMEM((nodes, 4 * slots), BF16),
            pltpu.VMEM((nodes, width), BF16),
            pltpu.VMEM((2, nodes, width), F32),
            pltpu.VMEM((nodes, 128), F32),
            pltpu.VMEM((LAYERS, 4, slots, width), BF16),
            pltpu.VMEM((LAYERS, 4, slots, width), BF16),
            pltpu.VMEM((ROUNDS, 4, 2, 128), F32),
            pltpu.VMEM((ROUNDS, 4, 2, 128), F32),
            pltpu.VMEM((n_dom, 1, 128), F32),
            pltpu.VMEM((n_sub, 1, 128), F32),
            dma((LAYERS, 4)),
            dma((LAYERS, 4)),
            dma((ROUNDS, 4)),
            dma((ROUNDS, 4)),
            dma((n_dom,)),
            dma((n_dom,)),
            dma((n_sub,)),
            dma((n_sub,)),
        ],
        compiler_params=pltpu.CompilerParams(
            collective_id=0, has_side_effects=True, vmem_limit_bytes=VMEM_BYTES
        ),
        name="solve",
    )(*copied)
    return heat[0], defect[0]


def solution(mesh):
    return jax.shard_map(
        functools.partial(per_device, mesh.shape["dom"], mesh.shape["sub"]),
        mesh=mesh,
        in_specs=(
            P(("dom", "sub"), None),
            P(("dom", "sub"), None, None, None),
            P(("dom", "sub"), None),
            P(("dom", "sub"), None),
            P(("dom", "sub")),
            P(("dom", "sub"), None, None),
            P(("dom", "sub"), None),
            P(("dom", "sub")),
            P(("dom", "sub")),
            P(),
            P(),
            P(),
            P(),
            P(),
            P(),
        ),
        out_specs=(P(("dom", "sub")), P(("dom", "sub"))),
        check_vma=False,
    )
```

```python
import functools

import jax
import jax.numpy as jnp
from jax import lax
from jax.experimental import pallas as pl
from jax.experimental.pallas import tpu as pltpu
from jax.sharding import PartitionSpec as P

LAYERS = 2
ITERS = 3
ROUNDS = ITERS + 1
VMEM_BYTES = 67_043_328
MESH = pl.DeviceIdType.MESH
F32 = jnp.float32
BF16 = jnp.bfloat16


def assemble(counts, rows, columns, tiles, chained, high, low):
    slots, size = tiles.shape[0], tiles.shape[1]
    groups = high.shape[0] // size
    spare = slots - groups
    chained[spare] = jnp.zeros((size, size), F32)
    keys = []
    for t in range(spare):
        r, c = rows[0, groups + t], columns[0, groups + t]
        key = jnp.where(
            groups + t < counts[0], jnp.minimum(r, c) * groups + jnp.maximum(r, c), -1
        )
        before = spare
        for u in range(t):
            before = jnp.where(keys[u] == key, u, before)
        keys.append(key)
        tile = tiles[groups + t]
        upright = jnp.where(r <= c, 1.0, 0.0)
        chained[t] = chained[before] + (upright * tile + (1.0 - upright) * tile.T)

    def put(i, j, block):
        upper = block.astype(BF16)
        at = (slice(i * size, (i + 1) * size), slice(j * size, (j + 1) * size))
        high[at] = upper
        low[at] = (block - upper.astype(F32)).astype(BF16)

    for i in range(groups):
        for j in range(i, groups):
            last = spare
            for u in range(spare):
                last = jnp.where(keys[u] == i * groups + j, u, last)
            block = chained[last]
            if i == j:
                block = block + tiles[i]
                put(i, i, block + block.T)
            else:
                put(i, j, block)
                put(j, i, block.T)


def dot(a, b):
    return jnp.dot(a, b, preferred_element_type=F32)


def parts_of(v):
    at = lax.broadcasted_iota(jnp.int32, v.shape, 0)
    first = v.astype(BF16).astype(F32)
    rest = v - first
    second = rest.astype(BF16).astype(F32)
    third = rest - second
    picked = jnp.where(at == 0, first, jnp.where(at == 1, second, jnp.where(at == 2, third, 0.0)))
    return picked.astype(BF16)


def joined(rows):
    return jnp.broadcast_to(jnp.sum(rows, axis=0, keepdims=True), rows.shape)


def spread(row):
    return jnp.broadcast_to(row, (8, row.shape[1]))


def rooted(v, gain):
    return v * lax.rsqrt(jnp.mean(v * v, axis=-1, keepdims=True) + 1e-06) * gain


def galerkin_weights(gram):
    matrix = [[gram(i, j) - gram(i, j + 1) for j in range(ITERS)] for i in range(ITERS)]
    right = [gram(i, 0) for i in range(ITERS)]
    for i in range(ITERS):
        for k in range(i + 1, ITERS):
            factor = matrix[i][k] / matrix[i][i]
            for j in range(k, ITERS):
                matrix[k][j] = matrix[k][j] - factor * matrix[i][j]
            right[k] = right[k] - factor * right[i]
    weights = [None] * ITERS
    for i in reversed(range(ITERS)):
        total = right[i]
        for j in range(i + 1, ITERS):
            total = total - matrix[i][j] * weights[j]
        weights[i] = total / matrix[i][i]
    return weights


def solve_kernel(n_dom, n_sub, *refs):
    copied, refs = refs[:15], refs[15:]
    (heat_ref, defect_ref), refs = refs[:2], refs[2:]
    local, refs = refs[:15], refs[15:]
    faces, send_ref, state, capacity, source, w_self, w_neighbour, w_out, gains, bias, w_decode = local[:11]
    tiles, rows, columns, counts = local[11:]
    (
        load,
        chained,
        high,
        low,
        pick,
        place,
        latents,
        own,
        inverse,
        diagonal_ref,
        row_out,
        row_in,
        face_out,
        face_in,
        dom_sums,
        sub_sums,
        row_send,
        row_recv,
        face_send,
        face_recv,
        dom_send,
        dom_recv,
        sub_send,
        sub_recv,
    ) = refs
    loads = [
        pltpu.make_async_copy(source_ref, target, load.at[n])
        for n, (source_ref, target) in enumerate(zip(copied, local))
    ]
    for n in (1, 0, 2, 12, 13, 14, 11, 5, 8, 9, 3, 6, 7, 10, 4):
        loads[n].start()
    dom, sub = lax.axis_index("dom"), lax.axis_index("sub")
    nodes, width = state.shape
    slots = send_ref.shape[1]
    chunk = 256
    sides = (
        (dom > 0, (dom - 1, sub)),
        (dom < n_dom - 1, (dom + 1, sub)),
        (sub > 0, (dom, sub - 1)),
        (sub < n_sub - 1, (dom, sub + 1)),
    )
    order = (2, 3, 1, 0)

    barrier = pltpu.get_barrier_semaphore()
    for r in range(1, n_dom):
        pl.semaphore_signal(barrier, inc=1, device_id=(lax.rem(dom + r, n_dom), sub), device_id_type=MESH)
    for r in range(1, n_sub):
        pl.semaphore_signal(barrier, inc=1, device_id=(dom, lax.rem(sub + r, n_sub)), device_id_type=MESH)

    position = lax.broadcasted_iota(jnp.int32, (8, slots), 1)
    loads[1].wait()
    loads[0].wait()
    wanted = [
        jnp.where(
            position < faces[0, k], jnp.broadcast_to(send_ref[k : k + 1, :], (8, slots)), -1
        ).astype(F32)
        for k in range(4)
    ]
    for k in order:
        node = lax.broadcasted_iota(jnp.int32, (slots, nodes), 1).astype(F32)
        upright = wanted[k].T[:, 0:1]
        pick[k * slots : (k + 1) * slots, :] = jnp.where(node == upright, 1.0, 0.0).astype(BF16)
    at_row = lax.broadcasted_iota(jnp.int32, (8, 128), 0)
    slot_node = jnp.zeros((8, 128), jnp.int32)
    for r in range(8):
        lanes = slice((r % 2) * 128, (r % 2) * 128 + 128)
        slot_node = jnp.where(at_row == r, send_ref[r // 2 : r // 2 + 1, lanes], slot_node)
    slot_lane, slot_group = jnp.bitwise_and(slot_node, 127), jnp.right_shift(slot_node, 7)
    loads[2].wait()

    for k, (there, _) in enumerate(sides):

        @pl.when(jnp.logical_not(there))
        def _():
            for layer in range(LAYERS):
                row_in[layer, k] = jnp.zeros((slots, width), BF16)
            for step in range(ROUNDS):
                face_in[step, k] = jnp.zeros((2, 128), F32)

    def row_copy(layer, k):
        return pltpu.make_async_remote_copy(
            src_ref=row_out.at[layer, k],
            dst_ref=row_in.at[layer, k ^ 1],
            send_sem=row_send.at[layer, k],
            recv_sem=row_recv.at[layer, k ^ 1],
            device_id=sides[k][1],
            device_id_type=MESH,
        )

    def row_arrival(layer, k):
        return pltpu.make_async_remote_copy(
            src_ref=row_out.at[layer, k],
            dst_ref=row_in.at[layer, k],
            send_sem=row_send.at[layer, k],
            recv_sem=row_recv.at[layer, k],
            device_id=sides[k][1],
            device_id_type=MESH,
        )

    def face_copy(step, k):
        return pltpu.make_async_remote_copy(
            src_ref=face_out.at[step, k],
            dst_ref=face_in.at[step, k ^ 1],
            send_sem=face_send.at[step, k],
            recv_sem=face_recv.at[step, k ^ 1],
            device_id=sides[k][1],
            device_id_type=MESH,
        )

    def face_arrival(step, k):
        return pltpu.make_async_remote_copy(
            src_ref=face_out.at[step, k],
            dst_ref=face_in.at[step, k],
            send_sem=face_send.at[step, k],
            recv_sem=face_recv.at[step, k],
            device_id=sides[k][1],
            device_id_type=MESH,
        )

    for layer in range(LAYERS):
        now = state if layer == 0 else latents
        for k in order:
            row_out[layer, k] = dot(pick[k * slots : (k + 1) * slots, :], now[...]).astype(BF16)
            if layer == 0 and k == order[0]:
                pl.semaphore_wait(barrier, n_dom + n_sub - 2)

            @pl.when(sides[k][0])
            def _():
                row_copy(layer, k).start()

        if layer == 0:
            for k in range(4):
                node = lax.broadcasted_iota(jnp.int32, (nodes, slots), 0).astype(F32)
                place[:, k * slots : (k + 1) * slots] = (
                    jnp.where(node == wanted[k][0:1, :], 1.0, 0.0).astype(BF16)
                )
            for n in range(3, len(loads)):
                loads[n].wait()
            assemble(counts, rows, columns, tiles, chained, high, low)
            ones = jnp.ones((8, nodes), BF16)
            rowsum = dot(ones, high[...]) + dot(ones, low[...]) + dot(ones, pick[...])
            flipped = 1.0 / rowsum
            for c in range(nodes // 128):
                at = slice(c * 128, (c + 1) * 128)
                inverse[at, :] = jnp.broadcast_to(flipped[:, at].T[:, 0:1], (128, 128))
            diagonal_ref[...] = spread(capacity[...]) + rowsum

        for b in range(nodes // chunk):
            at = slice(b * chunk, (b + 1) * chunk)
            normed = rooted(now[at, :].astype(F32), gains[layer, 0:1, :]).astype(BF16)
            own[1, at, :] = dot(normed, w_self[layer]) + bias[layer : layer + 1, :]
            own[0, at, :] = dot(high[at, :], now[...])

        def arrive(k):
            @pl.when(sides[k][0])
            def _():
                row_arrival(layer, k).wait_recv()

        arrived = row_in.at[layer]

        def side(k):
            for b in range(nodes // chunk):
                at = slice(b * chunk, (b + 1) * chunk)
                own[0, at, :] += dot(place[at, k * slots : (k + 1) * slots], arrived[k])

        for k in (0, 1):
            arrive(k)
            side(k)
        arrive(2)
        arrive(3)
        for b in range(nodes // chunk):
            at = slice(b * chunk, (b + 1) * chunk)
            coupled = own[0, at, :]
            for k in (2, 3):
                coupled = coupled + dot(place[at, k * slots : (k + 1) * slots], arrived[k])
            mean = coupled * jnp.concatenate([inverse[at, :]] * (width // 128), axis=1)
            normed = rooted(mean, gains[layer, 1:2, :]).astype(BF16)
            linear = own[1, at, :] + dot(normed, w_neighbour[layer])
            active = (linear / (1.0 + jnp.exp(-linear))).astype(BF16)
            latents[at, :] = (now[at, :].astype(F32) + dot(active, w_out[layer])).astype(BF16)

    guess = joined(
        lax.dot_general(
            parts_of(spread(w_decode[...])),
            latents[...],
            (((1,), (1,)), ((), ())),
            preferred_element_type=F32,
        )
    )
    diagonal = diagonal_ref[...]
    scaling = 1.0 / diagonal

    def couple(step, v):
        sent = jnp.zeros((8, 128), F32)
        for c in range(nodes // 128):
            found = jnp.take_along_axis(v[:, c * 128 : (c + 1) * 128], slot_lane, axis=1)
            sent = jnp.where(slot_group == c, found, sent)
        for k in order:
            face_out[step, k] = sent[2 * k : 2 * k + 2, :]

            @pl.when(sides[k][0])
            def _():
                face_copy(step, k).start()

        parts = parts_of(v)
        coupled = dot(parts, high[...]) + dot(parts, low[...])
        for k in range(4):

            @pl.when(sides[k][0])
            def _():
                face_arrival(step, k).wait_recv()

            came = face_in[step, k]
            came = jnp.concatenate([spread(came[0:1, :]), spread(came[1:2, :])], axis=1)
            coupled = coupled + dot(parts_of(came), pick[k * slots : (k + 1) * slots, :])
        return joined(coupled)

    first = scaling * (spread(source[...]) - (diagonal * guess - couple(0, guess)))
    basis = [first]
    for step in range(1, ROUNDS):
        basis.append(scaling * couple(step, basis[-1]))

    pairs = [(i, j) for i in range(ITERS) for j in range(i, ROUNDS)]
    at_row = lax.broadcasted_iota(jnp.int32, (16, 128), 0)
    at_lane = lax.broadcasted_iota(jnp.int32, (16, 128), 1)
    packed = jnp.zeros((16, 128), F32)
    weighted = [diagonal * v for v in basis]
    for n, (i, j) in enumerate(pairs):
        product = basis[i] * weighted[j]
        lanes = sum(product[0:1, c * 128 : (c + 1) * 128] for c in range(nodes // 128))
        packed = jnp.where(at_row == n, lanes, packed)
    packed = jnp.sum(packed, axis=1, keepdims=True)
    mine = jnp.sum(jnp.where(at_row == at_lane, packed, 0.0), axis=0, keepdims=True)

    dom_sums[dom] = mine

    def dom_copy(r):
        return pltpu.make_async_remote_copy(
            src_ref=dom_sums.at[dom],
            dst_ref=dom_sums.at[dom],
            send_sem=dom_send.at[r],
            recv_sem=dom_recv.at[r],
            device_id=(lax.rem(dom + r, n_dom), sub),
            device_id_type=MESH,
        )

    def sub_copy(r):
        return pltpu.make_async_remote_copy(
            src_ref=sub_sums.at[sub],
            dst_ref=sub_sums.at[sub],
            send_sem=sub_send.at[r],
            recv_sem=sub_recv.at[r],
            device_id=(dom, lax.rem(sub + r, n_sub)),
            device_id_type=MESH,
        )

    for r in sorted(range(1, n_dom), key=lambda r: -min(r, n_dom - r)):
        dom_copy(r).start()
    for r in range(1, n_dom):
        dom_copy(r).wait()
    sub_sums[sub] = jnp.sum(dom_sums[...], axis=0)
    for r in sorted(range(1, n_sub), key=lambda r: -min(r, n_sub - r)):
        sub_copy(r).start()
    for r in range(1, n_sub):
        sub_copy(r).wait()
    sums = jnp.sum(sub_sums[...], axis=0)

    lane = lax.broadcasted_iota(jnp.int32, (1, 128), 1)
    gram = {
        pair: jnp.sum(jnp.where(lane == n, sums, 0.0), axis=1, keepdims=True)
        for n, pair in enumerate(pairs)
    }
    weights = galerkin_weights(lambda i, j: gram[(min(i, j), max(i, j))])
    field, left = guess[0:1, :], basis[0][0:1, :]
    for step in range(ITERS):
        field = field + weights[step] * basis[step][0:1, :]
        left = left - weights[step] * (basis[step][0:1, :] - basis[step + 1][0:1, :])
    heat_ref[...] = field
    defect_ref[...] = diagonal[0:1, :] * left

    for k in order:

        @pl.when(sides[k][0])
        def _():
            for layer in range(LAYERS):
                row_copy(layer, k).wait_send()
            for step in range(ROUNDS):
                face_copy(step, k).wait_send()


def finish_kernel(heat, defect, heat_out, defect_out, sem):
    copies = [
        pltpu.make_async_copy(heat, heat_out, sem.at[0]),
        pltpu.make_async_copy(defect, defect_out, sem.at[1]),
    ]
    for copy in copies:
        copy.start()
    for copy in copies:
        copy.wait()


def finish(heat, defect):
    hbm = pl.BlockSpec(memory_space=pltpu.HBM)
    vmem = pl.BlockSpec(memory_space=pltpu.VMEM)
    heat, defect = pl.pallas_call(
        finish_kernel,
        out_shape=[jax.ShapeDtypeStruct(heat.shape, heat.dtype)] * 2,
        in_specs=[vmem, vmem],
        out_specs=[hbm, hbm],
        scratch_shapes=[pltpu.SemaphoreType.DMA((2,))],
        compiler_params=pltpu.CompilerParams(vmem_limit_bytes=VMEM_BYTES - (1 << 20)),
        name="finish",
    )(heat, defect)
    return heat[0], defect[0]


def per_device(
    n_dom,
    n_sub,
    state,
    tile_values,
    tile_rows,
    tile_columns,
    tile_counts,
    send_nodes,
    face_counts,
    capacity,
    source,
    w_self,
    w_neighbour,
    w_out,
    gains,
    bias,
    w_decode,
):
    nodes, width = state.shape
    slots = send_nodes.shape[2]
    tiles = tile_values[0]
    size = tiles.shape[1]
    hbm = pl.BlockSpec(memory_space=pltpu.HBM)
    vmem = pl.BlockSpec(memory_space=pltpu.VMEM)
    dma = pltpu.SemaphoreType.DMA
    copied = (
        face_counts,
        send_nodes[0],
        state,
        capacity[None, :],
        source[None, :],
        w_self,
        w_neighbour,
        w_out,
        gains,
        bias,
        w_decode[None, :],
        tiles,
        tile_rows,
        tile_columns,
        tile_counts,
    )
    in_smem = (face_counts, tile_rows, tile_columns, tile_counts)
    heat, defect = pl.pallas_call(
        functools.partial(solve_kernel, n_dom, n_sub),
        out_shape=[jax.ShapeDtypeStruct((1, nodes), F32)] * 2,
        in_specs=[hbm] * len(copied),
        out_specs=[vmem, vmem],
        scratch_shapes=[
            (pltpu.SMEM if any(array is one for one in in_smem) else pltpu.VMEM)(
                array.shape, array.dtype
            )
            for array in copied
        ]
        + [
            dma((len(copied),)),
            pltpu.VMEM((tiles.shape[0] - nodes // size + 1, size, size), F32),
            pltpu.VMEM((nodes, nodes), BF16),
            pltpu.VMEM((nodes, nodes), BF16),
            pltpu.VMEM((4 * slots, nodes), BF16),
            pltpu.VMEM((nodes, 4 * slots), BF16),
            pltpu.VMEM((nodes, width), BF16),
            pltpu.VMEM((2, nodes, width), F32),
            pltpu.VMEM((nodes, 128), F32),
            pltpu.VMEM((8, nodes), F32),
            pltpu.VMEM((LAYERS, 4, slots, width), BF16),
            pltpu.VMEM((LAYERS, 4, slots, width), BF16),
            pltpu.VMEM((ROUNDS, 4, 2, 128), F32),
            pltpu.VMEM((ROUNDS, 4, 2, 128), F32),
            pltpu.VMEM((n_dom, 1, 128), F32),
            pltpu.VMEM((n_sub, 1, 128), F32),
            dma((LAYERS, 4)),
            dma((LAYERS, 4)),
            dma((ROUNDS, 4)),
            dma((ROUNDS, 4)),
            dma((n_dom,)),
            dma((n_dom,)),
            dma((n_sub,)),
            dma((n_sub,)),
        ],
        compiler_params=pltpu.CompilerParams(
            collective_id=0, has_side_effects=True, vmem_limit_bytes=VMEM_BYTES - 16384
        ),
        name="solve",
    )(*copied)
    return finish(heat, defect)


def solution(mesh):
    return jax.shard_map(
        functools.partial(per_device, mesh.shape["dom"], mesh.shape["sub"]),
        mesh=mesh,
        in_specs=(
            P(("dom", "sub"), None),
            P(("dom", "sub"), None, None, None),
            P(("dom", "sub"), None),
            P(("dom", "sub"), None),
            P(("dom", "sub")),
            P(("dom", "sub"), None, None),
            P(("dom", "sub"), None),
            P(("dom", "sub")),
            P(("dom", "sub")),
            P(),
            P(),
            P(),
            P(),
            P(),
            P(),
        ),
        out_specs=(P(("dom", "sub")), P(("dom", "sub"))),
        check_vma=False,
    )
```

```python
import functools

import jax
import jax.numpy as jnp
from jax import lax
from jax.experimental import pallas as pl
from jax.experimental.pallas import tpu as pltpu
from jax.sharding import PartitionSpec as P

LAYERS = 2
ITERS = 3
ROUNDS = ITERS + 1
VMEM_BYTES = 67_043_328
MESH = pl.DeviceIdType.MESH
F32 = jnp.float32
BF16 = jnp.bfloat16


def assemble(counts, rows, columns, tiles, chained, high, low):
    slots, size = tiles.shape[0], tiles.shape[1]
    groups = high.shape[0] // size
    spare = slots - groups
    chained[spare] = jnp.zeros((size, size), F32)
    keys = []
    for t in range(spare):
        r, c = rows[0, groups + t], columns[0, groups + t]
        key = jnp.where(
            groups + t < counts[0], jnp.minimum(r, c) * groups + jnp.maximum(r, c), -1
        )
        before = spare
        for u in range(t):
            before = jnp.where(keys[u] == key, u, before)
        keys.append(key)
        tile = tiles[groups + t]
        upright = jnp.where(r <= c, 1.0, 0.0)
        chained[t] = chained[before] + (upright * tile + (1.0 - upright) * tile.T)

    def put(i, j, block):
        upper = block.astype(BF16)
        at = (slice(i * size, (i + 1) * size), slice(j * size, (j + 1) * size))
        high[at] = upper
        low[at] = (block - upper.astype(F32)).astype(BF16)

    for i in range(groups):
        for j in range(i, groups):
            last = spare
            for u in range(spare):
                last = jnp.where(keys[u] == i * groups + j, u, last)
            block = chained[last]
            if i == j:
                block = block + tiles[i]
                put(i, i, block + block.T)
            else:
                put(i, j, block)
                put(j, i, block.T)


def dot(a, b):
    return jnp.dot(a, b, preferred_element_type=F32)


def parts_of(v):
    at = lax.broadcasted_iota(jnp.int32, v.shape, 0)
    first = v.astype(BF16).astype(F32)
    rest = v - first
    second = rest.astype(BF16).astype(F32)
    third = rest - second
    picked = jnp.where(at == 0, first, jnp.where(at == 1, second, jnp.where(at == 2, third, 0.0)))
    return picked.astype(BF16)


def joined(rows):
    return jnp.broadcast_to(jnp.sum(rows, axis=0, keepdims=True), rows.shape)


def spread(row):
    return jnp.broadcast_to(row, (8, row.shape[1]))


def rooted(v, gain):
    return v * lax.rsqrt(jnp.mean(v * v, axis=-1, keepdims=True) + 1e-06) * gain


def galerkin_weights(gram):
    matrix = [[gram(i, j) - gram(i, j + 1) for j in range(ITERS)] for i in range(ITERS)]
    right = [gram(i, 0) for i in range(ITERS)]
    for i in range(ITERS):
        for k in range(i + 1, ITERS):
            factor = matrix[i][k] / matrix[i][i]
            for j in range(k, ITERS):
                matrix[k][j] = matrix[k][j] - factor * matrix[i][j]
            right[k] = right[k] - factor * right[i]
    weights = [None] * ITERS
    for i in reversed(range(ITERS)):
        total = right[i]
        for j in range(i + 1, ITERS):
            total = total - matrix[i][j] * weights[j]
        weights[i] = total / matrix[i][i]
    return weights


def solve_kernel(n_dom, n_sub, *refs):
    copied, refs = refs[:15], refs[15:]
    (heat_ref, defect_ref), refs = refs[:2], refs[2:]
    local, refs = refs[:15], refs[15:]
    faces, send_ref, state, capacity, source, w_self, w_neighbour, w_out, gains, bias, w_decode = local[:11]
    tiles, rows, columns, counts = local[11:]
    (
        load,
        chained,
        high,
        low,
        pick,
        place,
        latents,
        own,
        inverse,
        diagonal_ref,
        row_out,
        row_in,
        face_out,
        face_in,
        dom_sums,
        sub_sums,
        row_send,
        row_recv,
        face_send,
        face_recv,
        dom_send,
        dom_recv,
        sub_send,
        sub_recv,
    ) = refs
    loads = [
        pltpu.make_async_copy(source_ref, target, load.at[n])
        for n, (source_ref, target) in enumerate(zip(copied, local))
    ]
    for n in (1, 0, 2, 12, 13, 14, 11, 5, 8, 9, 3, 6, 7, 10, 4):
        loads[n].start()
    dom, sub = lax.axis_index("dom"), lax.axis_index("sub")
    nodes, width = state.shape
    slots = send_ref.shape[1]
    chunk = 512
    sides = (
        (dom > 0, (dom - 1, sub)),
        (dom < n_dom - 1, (dom + 1, sub)),
        (sub > 0, (dom, sub - 1)),
        (sub < n_sub - 1, (dom, sub + 1)),
    )
    order = (2, 3, 1, 0)

    barrier = pltpu.get_barrier_semaphore()
    for r in range(1, n_dom):
        pl.semaphore_signal(barrier, inc=1, device_id=(lax.rem(dom + r, n_dom), sub), device_id_type=MESH)
    for r in range(1, n_sub):
        pl.semaphore_signal(barrier, inc=1, device_id=(dom, lax.rem(sub + r, n_sub)), device_id_type=MESH)

    position = lax.broadcasted_iota(jnp.int32, (8, slots), 1)
    loads[1].wait()
    loads[0].wait()
    wanted = [
        jnp.where(
            position < faces[0, k], jnp.broadcast_to(send_ref[k : k + 1, :], (8, slots)), -1
        ).astype(F32)
        for k in range(4)
    ]
    for k in order:
        node = lax.broadcasted_iota(jnp.int32, (slots, nodes), 1).astype(F32)
        upright = wanted[k].T[:, 0:1]
        pick[k * slots : (k + 1) * slots, :] = jnp.where(node == upright, 1.0, 0.0).astype(BF16)
    at_row = lax.broadcasted_iota(jnp.int32, (8, 128), 0)
    slot_node = jnp.zeros((8, 128), jnp.int32)
    for r in range(8):
        lanes = slice((r % 2) * 128, (r % 2) * 128 + 128)
        slot_node = jnp.where(at_row == r, send_ref[r // 2 : r // 2 + 1, lanes], slot_node)
    slot_lane, slot_group = jnp.bitwise_and(slot_node, 127), jnp.right_shift(slot_node, 7)
    loads[2].wait()

    for k, (there, _) in enumerate(sides):

        @pl.when(jnp.logical_not(there))
        def _():
            for layer in range(LAYERS):
                row_in[layer, k] = jnp.zeros((slots, width), BF16)
            for step in range(ROUNDS):
                face_in[step, k] = jnp.zeros((2, 128), F32)

    def row_copy(layer, k):
        return pltpu.make_async_remote_copy(
            src_ref=row_out.at[layer, k],
            dst_ref=row_in.at[layer, k ^ 1],
            send_sem=row_send.at[layer, k],
            recv_sem=row_recv.at[layer, k ^ 1],
            device_id=sides[k][1],
            device_id_type=MESH,
        )

    def row_arrival(layer, k):
        return pltpu.make_async_remote_copy(
            src_ref=row_out.at[layer, k],
            dst_ref=row_in.at[layer, k],
            send_sem=row_send.at[layer, k],
            recv_sem=row_recv.at[layer, k],
            device_id=sides[k][1],
            device_id_type=MESH,
        )

    def face_copy(step, k):
        return pltpu.make_async_remote_copy(
            src_ref=face_out.at[step, k],
            dst_ref=face_in.at[step, k ^ 1],
            send_sem=face_send.at[step, k],
            recv_sem=face_recv.at[step, k ^ 1],
            device_id=sides[k][1],
            device_id_type=MESH,
        )

    def face_arrival(step, k):
        return pltpu.make_async_remote_copy(
            src_ref=face_out.at[step, k],
            dst_ref=face_in.at[step, k],
            send_sem=face_send.at[step, k],
            recv_sem=face_recv.at[step, k],
            device_id=sides[k][1],
            device_id_type=MESH,
        )

    for layer in range(LAYERS):
        now = state if layer == 0 else latents
        for k in order:
            row_out[layer, k] = dot(pick[k * slots : (k + 1) * slots, :], now[...]).astype(BF16)
            if layer == 0 and k == order[0]:
                pl.semaphore_wait(barrier, n_dom + n_sub - 2)

            @pl.when(sides[k][0])
            def _():
                row_copy(layer, k).start()

        if layer == 0:
            for k in range(4):
                node = lax.broadcasted_iota(jnp.int32, (nodes, slots), 0).astype(F32)
                place[:, k * slots : (k + 1) * slots] = (
                    jnp.where(node == wanted[k][0:1, :], 1.0, 0.0).astype(BF16)
                )
            for n in range(3, len(loads)):
                loads[n].wait()
            assemble(counts, rows, columns, tiles, chained, high, low)
            ones = jnp.ones((8, nodes), BF16)
            rowsum = dot(ones, high[...]) + dot(ones, low[...]) + dot(ones, pick[...])
            flipped = 1.0 / rowsum
            for c in range(nodes // 128):
                at = slice(c * 128, (c + 1) * 128)
                inverse[at, :] = jnp.broadcast_to(flipped[:, at].T[:, 0:1], (128, 128))
            diagonal_ref[...] = spread(capacity[...]) + rowsum

        for b in range(nodes // chunk):
            at = slice(b * chunk, (b + 1) * chunk)
            normed = rooted(now[at, :].astype(F32), gains[layer, 0:1, :]).astype(BF16)
            own[1, at, :] = dot(normed, w_self[layer]) + bias[layer : layer + 1, :]
            own[0, at, :] = dot(high[at, :], now[...])

        def arrive(k):
            @pl.when(sides[k][0])
            def _():
                row_arrival(layer, k).wait_recv()

        arrived = row_in.at[layer]

        def side(k):
            for b in range(nodes // chunk):
                at = slice(b * chunk, (b + 1) * chunk)
                own[0, at, :] += dot(place[at, k * slots : (k + 1) * slots], arrived[k])

        for k in (0, 1):
            arrive(k)
            side(k)
        arrive(2)
        arrive(3)
        for b in range(nodes // chunk):
            at = slice(b * chunk, (b + 1) * chunk)
            coupled = own[0, at, :]
            for k in (2, 3):
                coupled = coupled + dot(place[at, k * slots : (k + 1) * slots], arrived[k])
            mean = coupled * jnp.concatenate([inverse[at, :]] * (width // 128), axis=1)
            normed = rooted(mean, gains[layer, 1:2, :]).astype(BF16)
            linear = own[1, at, :] + dot(normed, w_neighbour[layer])
            active = (linear / (1.0 + jnp.exp(-linear))).astype(BF16)
            latents[at, :] = (now[at, :].astype(F32) + dot(active, w_out[layer])).astype(BF16)

    guess = joined(
        lax.dot_general(
            parts_of(spread(w_decode[...])),
            latents[...],
            (((1,), (1,)), ((), ())),
            preferred_element_type=F32,
        )
    )
    diagonal = diagonal_ref[...]
    scaling = 1.0 / diagonal

    def couple(step, v):
        sent = jnp.zeros((8, 128), F32)
        for c in range(nodes // 128):
            found = jnp.take_along_axis(v[:, c * 128 : (c + 1) * 128], slot_lane, axis=1)
            sent = jnp.where(slot_group == c, found, sent)
        for k in order:
            face_out[step, k] = sent[2 * k : 2 * k + 2, :]

            @pl.when(sides[k][0])
            def _():
                face_copy(step, k).start()

        parts = parts_of(v)
        coupled = dot(parts, high[...]) + dot(parts, low[...])
        for k in range(4):

            @pl.when(sides[k][0])
            def _():
                face_arrival(step, k).wait_recv()

            came = face_in[step, k]
            came = jnp.concatenate([spread(came[0:1, :]), spread(came[1:2, :])], axis=1)
            coupled = coupled + dot(parts_of(came), pick[k * slots : (k + 1) * slots, :])
        return joined(coupled)

    first = scaling * (spread(source[...]) - (diagonal * guess - couple(0, guess)))
    basis = [first]
    for step in range(1, ROUNDS):
        basis.append(scaling * couple(step, basis[-1]))

    pairs = [(i, j) for i in range(ITERS) for j in range(i, ROUNDS)]
    at_row = lax.broadcasted_iota(jnp.int32, (16, 128), 0)
    at_lane = lax.broadcasted_iota(jnp.int32, (16, 128), 1)
    packed = jnp.zeros((16, 128), F32)
    weighted = [diagonal * v for v in basis]
    for n, (i, j) in enumerate(pairs):
        product = basis[i] * weighted[j]
        lanes = sum(product[0:1, c * 128 : (c + 1) * 128] for c in range(nodes // 128))
        packed = jnp.where(at_row == n, lanes, packed)
    packed = jnp.sum(packed, axis=1, keepdims=True)
    mine = jnp.sum(jnp.where(at_row == at_lane, packed, 0.0), axis=0, keepdims=True)

    dom_sums[dom] = mine

    def dom_copy(r):
        return pltpu.make_async_remote_copy(
            src_ref=dom_sums.at[dom],
            dst_ref=dom_sums.at[dom],
            send_sem=dom_send.at[r],
            recv_sem=dom_recv.at[r],
            device_id=(lax.rem(dom + r, n_dom), sub),
            device_id_type=MESH,
        )

    def sub_copy(r):
        return pltpu.make_async_remote_copy(
            src_ref=sub_sums.at[sub],
            dst_ref=sub_sums.at[sub],
            send_sem=sub_send.at[r],
            recv_sem=sub_recv.at[r],
            device_id=(dom, lax.rem(sub + r, n_sub)),
            device_id_type=MESH,
        )

    for r in sorted(range(1, n_dom), key=lambda r: -min(r, n_dom - r)):
        dom_copy(r).start()
    for r in range(1, n_dom):
        dom_copy(r).wait_recv()
    sub_sums[sub] = jnp.sum(dom_sums[...], axis=0)
    for r in sorted(range(1, n_sub), key=lambda r: -min(r % 4, 4 - r % 4) - min(r // 4, 4 - r // 4)):
        sub_copy(r).start()
    for r in range(1, n_sub):
        sub_copy(r).wait_recv()
    sums = jnp.sum(sub_sums[...], axis=0)

    lane = lax.broadcasted_iota(jnp.int32, (1, 128), 1)
    gram = {
        pair: jnp.sum(jnp.where(lane == n, sums, 0.0), axis=1, keepdims=True)
        for n, pair in enumerate(pairs)
    }
    weights = galerkin_weights(lambda i, j: gram[(min(i, j), max(i, j))])
    field, left = guess[0:1, :], basis[0][0:1, :]
    for step in range(ITERS):
        field = field + weights[step] * basis[step][0:1, :]
        left = left - weights[step] * (basis[step][0:1, :] - basis[step + 1][0:1, :])
    for r in range(1, n_dom):
        dom_copy(r).wait_send()
    for r in range(1, n_sub):
        sub_copy(r).wait_send()
    heat_ref[...] = field
    defect_ref[...] = diagonal[0:1, :] * left

    for k in order:

        @pl.when(sides[k][0])
        def _():
            for layer in range(LAYERS):
                row_copy(layer, k).wait_send()
            for step in range(ROUNDS):
                face_copy(step, k).wait_send()


def finish_kernel(heat, defect, heat_out, defect_out, sem):
    copies = [
        pltpu.make_async_copy(heat, heat_out, sem.at[0]),
        pltpu.make_async_copy(defect, defect_out, sem.at[1]),
    ]
    for copy in copies:
        copy.start()
    for copy in copies:
        copy.wait()


def finish(heat, defect):
    hbm = pl.BlockSpec(memory_space=pltpu.HBM)
    vmem = pl.BlockSpec(memory_space=pltpu.VMEM)
    heat, defect = pl.pallas_call(
        finish_kernel,
        out_shape=[jax.ShapeDtypeStruct(heat.shape, heat.dtype)] * 2,
        in_specs=[vmem, vmem],
        out_specs=[hbm, hbm],
        scratch_shapes=[pltpu.SemaphoreType.DMA((2,))],
        compiler_params=pltpu.CompilerParams(vmem_limit_bytes=VMEM_BYTES - (1 << 20)),
        name="finish",
    )(heat, defect)
    return heat[0], defect[0]


def per_device(
    n_dom,
    n_sub,
    state,
    tile_values,
    tile_rows,
    tile_columns,
    tile_counts,
    send_nodes,
    face_counts,
    capacity,
    source,
    w_self,
    w_neighbour,
    w_out,
    gains,
    bias,
    w_decode,
):
    nodes, width = state.shape
    slots = send_nodes.shape[2]
    tiles = tile_values[0]
    size = tiles.shape[1]
    hbm = pl.BlockSpec(memory_space=pltpu.HBM)
    vmem = pl.BlockSpec(memory_space=pltpu.VMEM)
    dma = pltpu.SemaphoreType.DMA
    copied = (
        face_counts,
        send_nodes[0],
        state,
        capacity[None, :],
        source[None, :],
        w_self,
        w_neighbour,
        w_out,
        gains,
        bias,
        w_decode[None, :],
        tiles,
        tile_rows,
        tile_columns,
        tile_counts,
    )
    in_smem = (face_counts, tile_rows, tile_columns, tile_counts)
    heat, defect = pl.pallas_call(
        functools.partial(solve_kernel, n_dom, n_sub),
        out_shape=[jax.ShapeDtypeStruct((1, nodes), F32)] * 2,
        in_specs=[hbm] * len(copied),
        out_specs=[vmem, vmem],
        scratch_shapes=[
            (pltpu.SMEM if any(array is one for one in in_smem) else pltpu.VMEM)(
                array.shape, array.dtype
            )
            for array in copied
        ]
        + [
            dma((len(copied),)),
            pltpu.VMEM((tiles.shape[0] - nodes // size + 1, size, size), F32),
            pltpu.VMEM((nodes, nodes), BF16),
            pltpu.VMEM((nodes, nodes), BF16),
            pltpu.VMEM((4 * slots, nodes), BF16),
            pltpu.VMEM((nodes, 4 * slots), BF16),
            pltpu.VMEM((nodes, width), BF16),
            pltpu.VMEM((2, nodes, width), F32),
            pltpu.VMEM((nodes, 128), F32),
            pltpu.VMEM((8, nodes), F32),
            pltpu.VMEM((LAYERS, 4, slots, width), BF16),
            pltpu.VMEM((LAYERS, 4, slots, width), BF16),
            pltpu.VMEM((ROUNDS, 4, 2, 128), F32),
            pltpu.VMEM((ROUNDS, 4, 2, 128), F32),
            pltpu.VMEM((n_dom, 1, 128), F32),
            pltpu.VMEM((n_sub, 1, 128), F32),
            dma((LAYERS, 4)),
            dma((LAYERS, 4)),
            dma((ROUNDS, 4)),
            dma((ROUNDS, 4)),
            dma((n_dom,)),
            dma((n_dom,)),
            dma((n_sub,)),
            dma((n_sub,)),
        ],
        compiler_params=pltpu.CompilerParams(
            collective_id=0, has_side_effects=True, vmem_limit_bytes=VMEM_BYTES - 16384
        ),
        name="solve",
    )(*copied)
    return finish(heat, defect)


def solution(mesh):
    return jax.shard_map(
        functools.partial(per_device, mesh.shape["dom"], mesh.shape["sub"]),
        mesh=mesh,
        in_specs=(
            P(("dom", "sub"), None),
            P(("dom", "sub"), None, None, None),
            P(("dom", "sub"), None),
            P(("dom", "sub"), None),
            P(("dom", "sub")),
            P(("dom", "sub"), None, None),
            P(("dom", "sub"), None),
            P(("dom", "sub")),
            P(("dom", "sub")),
            P(),
            P(),
            P(),
            P(),
            P(),
            P(),
        ),
        out_specs=(P(("dom", "sub")), P(("dom", "sub"))),
        check_vma=False,
    )
```
